512 devices in a mesh: lat: 32 (over x, z_hi, core), lev: 16 (over z_lo, y).
Axes of the slice: x: 4, y: 8, z: 8 (z_hi: 4, z_lo: 2; z = z_hi * 2 + z_lo), core: 2. Of those that a mesh axis runs over, the one named last changes fastest.
Arguments:
- thickness: float32 [64, 1024, 1152], P('lev', 'lat'), may hold values from 0.5 to 1.5
- tracer_mass: float32 [64, 1024, 1152], P('lev', 'lat'), may hold values from -6 to 6
- courant_lon: float32 [64, 1024, 1152], P('lev', 'lat'), may hold values from -0.12 to 0.12
- courant_lat: float32 [64, 1024, 1152], P('lev', 'lat'), may hold values from -0.12 to 0.12
- filter_cut: int32 [1024], P('lat'), may hold values from 4 to 576, as said below
- target_weights: int32 [64, 1024, 1152], P(None, 'lat', 'lev'), may hold values from 1 to 8
Outputs:
- remapped_thickness: float32 [64, 1024, 1152], P(None, 'lat', 'lev')
- remapped_tracer: float32 [64, 1024, 1152], P(None, 'lat', 'lev')
The draws below stay inside these ranges and needn't reach their ends.
Inputs may be any that keep to these rules, and one draw needn't show every extreme that they name: filter_cut is 576 on every row outside the first 64 and the last 64 latitude rows; inside them it is at least 4.
All inputs are finite; a program needn't handle non-finite values.
Results may differ from the reference program's by a relative error of at most 0.0003.
Values sent between devices are 32-bit elements; how exact they have to be, the bound alone decides.
A program may use at most 64 MiB of HBM per device.

```python
import jax
import jax.numpy as jnp
from jax import lax

NLON = 1152
ITERS = 2
NLAT = 1024
NLEV = 64
POLAR = 64


def draw_filter_cut(key, part):
    row_index = jnp.arange(NLAT)
    polar_rows = (row_index < POLAR) | (row_index >= NLAT - POLAR)
    cut_values = jax.random.randint(key, (NLAT,), 4, NLON // 2)
    cut_values = jnp.where(row_index == 0, 4, cut_values)
    return jnp.where(polar_rows, cut_values, NLON // 2).astype(jnp.int32)


def plant(entries, rng, least, high):
    spot = [jax.random.randint(jax.random.fold_in(rng, axis), (), 0, length) for axis, length in enumerate(entries.shape)]
    main_axis = entries.shape.index(max(entries.shape))
    beside = spot[:main_axis] + [(spot[main_axis] + 1) % entries.shape[main_axis]] + spot[main_axis + 1:]
    return entries.at[tuple(spot)].set(least).at[tuple(beside)].set(high)


def block_levels(own_key, extent, split, smallest, top_value):
    gain = 1.0
    for position, parts in split:
        draws = jax.random.uniform(jax.random.fold_in(jax.random.fold_in(own_key, 6), position), (parts,), jnp.float32, smallest / len(split), top_value / len(split))
        gain = gain * jnp.repeat(jnp.exp(draws), extent[position] // parts).reshape((-1,) + (1,) * (len(extent) - 1 - position))
    return gain


def scatter_about(rng, shape, deviation, most, split=(), kind=jnp.bfloat16):
    factor_of = block_levels(rng, shape, split, -0.22, 0.18) if split else 1.0
    result = jax.random.normal(rng, shape, jnp.float32) * deviation * factor_of
    return jnp.minimum(jnp.maximum(result, -most), most).astype(kind)


def setup_inputs(seed: int = 0) -> dict:
    key_list = jax.random.split(jax.random.key(seed), 7)
    thickness = jnp.clip(0.5 + 1.0 * jax.random.uniform(key_list[0], (NLEV, NLAT, NLON), jnp.float32) ** block_levels(key_list[0], (NLEV, NLAT, NLON), ((0, 16), (1, 32)), -0.2, 0.2), 0.5, 1.5)
    tracer_mass = scatter_about(key_list[1], (NLEV, NLAT, NLON), 1.0, 6.0, ((0, 16), (1, 32)), jnp.float32)
    courant_lon = jnp.clip(jax.random.uniform(key_list[2], (NLEV, NLAT, NLON), jnp.float32, -0.12, 0.12) * block_levels(key_list[2], (NLEV, NLAT, NLON), ((0, 16), (1, 32)), -0.4, 0.0), -0.12, 0.12)
    courant_lat = jnp.clip(jax.random.uniform(key_list[3], (NLEV, NLAT, NLON), jnp.float32, -0.12, 0.12) * block_levels(key_list[3], (NLEV, NLAT, NLON), ((0, 16), (1, 32)), -0.4, 0.0), -0.12, 0.12)
    filter_cut = draw_filter_cut(jax.random.fold_in(key_list[6], 71), 0)
    target_weights = plant(jax.random.randint(key_list[5], (NLEV, NLAT, NLON), 1, 9), jax.random.fold_in(key_list[5], 1), 1, 8).astype(jnp.int32)
    return dict(thickness=thickness, tracer_mass=tracer_mass, courant_lon=courant_lon, courant_lat=courant_lat, filter_cut=filter_cut, target_weights=target_weights)


def advance(fields, courant_x, courant_y, first_row, lat_total):
    row_count = courant_y.shape[1] - 2
    courant_core = courant_x[:, 1:-1]
    face_courant = 0.5 * (courant_y[:, :-1] + courant_y[:, 1:])
    face_index = first_row - 1 + jnp.arange(row_count + 1, dtype=jnp.int32)
    face_cos = jnp.sin(jnp.pi * jnp.minimum(face_index + 1, lat_total - face_index - 1).astype(jnp.float32) / lat_total)
    cell_index = first_row + jnp.arange(row_count, dtype=jnp.int32)
    cell_cos = jnp.sin(jnp.pi * (cell_index.astype(jnp.float32) + 0.5) / lat_total)
    results = []
    for field_now in fields:
        core_rows = field_now[:, 1:-1]
        upwind_lon = jnp.where(courant_core >= 0, core_rows, jnp.roll(core_rows, -1, axis=2))
        lon_flux = courant_core * upwind_lon
        upwind_lat = jnp.where(face_courant >= 0, field_now[:, :-1], field_now[:, 1:])
        lat_flux = face_courant * upwind_lat * face_cos[None, :, None]
        results.append(core_rows - (lon_flux - jnp.roll(lon_flux, 1, axis=2)) - (lat_flux[:, 1:] - lat_flux[:, :-1]) / cell_cos[None, :, None])
    return tuple(results)


def remap_columns(thick_cols, tracer_cols, weight_cols):
    level_total = thick_cols.shape[0]
    running_sum = jnp.cumsum(thick_cols, axis=0)
    zero_row = jnp.zeros((1, thick_cols.shape[1]), jnp.float32)
    layer_tops = jnp.concatenate([zero_row, running_sum[:-1]], axis=0)
    column_mass = running_sum[-1]
    weight_sums = jnp.cumsum(weight_cols, axis=0)
    fraction = weight_sums.astype(jnp.float32) / weight_sums[-1:].astype(jnp.float32)
    targets = column_mass[None, :] * fraction
    target_blocks = targets.reshape(level_total // 8, 8, thick_cols.shape[1])

    def accumulate(block_now):
        share = jnp.clip((block_now[:, None, :] - layer_tops[None]) / thick_cols[None], 0.0, 1.0)
        return jnp.sum(share * tracer_cols[None], axis=1)

    mass_below = lax.map(accumulate, target_blocks).reshape(level_total, thick_cols.shape[1])
    new_thickness = targets - jnp.concatenate([zero_row, targets[:-1]], axis=0)
    new_tracer = mass_below - jnp.concatenate([zero_row, mass_below[:-1]], axis=0)
    return new_thickness, new_tracer


def pad_rows(values):
    return jnp.pad(values, ((0, 0), (1, 1), (0, 0)))


def reference(thickness, tracer_mass, courant_lon, courant_lat, filter_cut, target_weights):
    fields = (thickness, tracer_mass)
    padded_x = pad_rows(courant_lon)
    padded_y = pad_rows(courant_lat)
    for substep in range(ITERS):
        fields = advance((pad_rows(fields[0]), pad_rows(fields[1])), padded_x, padded_y, 0, NLAT)
    tendency = fields[1] - tracer_mass
    spectrum = jnp.fft.rfft(tendency, axis=2)
    wave_index = jnp.arange(NLON // 2 + 1, dtype=jnp.int32)
    cut_ratio = filter_cut.astype(jnp.float32)[:, None] / jnp.maximum(wave_index, 1).astype(jnp.float32)[None, :]
    damping = jnp.where(wave_index[None, :] == 0, 1.0, jnp.minimum(1.0, cut_ratio * cut_ratio))
    filtered = jnp.fft.irfft(spectrum * damping[None], n=NLON, axis=2).astype(jnp.float32)
    tracer_final = tracer_mass + filtered

    def one_row(packed):
        return remap_columns(packed[0], packed[1], packed[2])

    new_thickness, new_tracer = lax.map(one_row, (jnp.moveaxis(fields[0], 1, 0), jnp.moveaxis(tracer_final, 1, 0), jnp.moveaxis(target_weights, 1, 0)))
    return jnp.moveaxis(new_thickness, 0, 1), jnp.moveaxis(new_tracer, 0, 1)
```

```python
import functools

import jax
import jax.numpy as jnp
import ml_dtypes
import numpy as np
from jax import lax
from jax.experimental import pallas as pl
from jax.experimental.pallas import tpu as pltpu
from jax.sharding import PartitionSpec as P

ITERS = 2
LANES = 128
MESH = pl.DeviceIdType.MESH


def split_bf16(table):
    high = table.astype(ml_dtypes.bfloat16)
    low = (table - high.astype(np.float64)).astype(ml_dtypes.bfloat16)
    return high, low


def fourier_tables(lon):
    half = lon // 2
    quarter = half // 2
    index = np.arange(half)
    even_wave = np.where(index <= quarter, 2 * index, 2 * (index - quarter))
    even_sine = index > quarter
    odd_wave = np.where(index < quarter, 2 * index + 1, 2 * (index - quarter) + 1)
    odd_sine = index >= quarter
    parts = []
    inverse = []
    for wave, sine in ((even_wave, even_sine), (odd_wave, odd_sine)):
        phase = 2.0 * np.pi / lon * (wave[:, None] * index[None, :] % lon)
        basis = np.where(sine[:, None], np.sin(phase), np.cos(phase))
        scale = np.where((wave == 0) | (wave == half), 1.0 / lon, 2.0 / lon)
        parts.append(basis)
        inverse.append((basis * scale[:, None]).T)
    forward_high, forward_low = split_bf16(np.stack(parts))
    inverse_high, inverse_low = split_bf16(np.stack(inverse))
    return np.stack([forward_high, forward_low, inverse_high, inverse_low])


def face_cosine(row, lat_total):
    return jnp.sin(jnp.pi / lat_total * jnp.minimum(row + 1, lat_total - row - 1).astype(jnp.float32))


def cell_cosine(row, lat_total):
    return jnp.sin(jnp.pi / lat_total * (row.astype(jnp.float32) + 0.5))


def advance(field, north, flux_south, lon_pos, lon_neg, lat_pos, lat_neg, inv_cos):
    width = field.shape[1]
    east = pltpu.roll(field, width - 1, axis=1)
    lon_flux = lon_pos * field + lon_neg * east
    lat_flux = lat_pos * field + lat_neg * north
    south = flux_south(lat_flux)
    return field - (lon_flux - pltpu.roll(lon_flux, 1, axis=1)) - (lat_flux - south) * inv_cos


def move_kernel(
    n_lat, n_lev, lat_total,
    thick_in, tracer_in, lon_in, lat_in, cut_in, tables_in,
    thick_out, tracer_out,
    pack, halo, edge_first, thick_rows, tracer_rows, tend_rows, thick_send, tracer_send, tend_cols, cut_lanes, tables,
    halo_sent, halo_got, thick_sent, thick_got, tracer_sent, tracer_got, table_sem,
):
    levels, rows, width = thick_in.shape
    dest = width // n_lev
    lat = lax.axis_index("lat")
    lev = lax.axis_index("lev")
    north = lax.rem(lat + 1, n_lat)
    south = lax.rem(lat + n_lat - 1, n_lat)
    polar = (lat < 2) | (lat >= n_lat - 2)
    barrier = pltpu.get_barrier_semaphore()
    for place in (north, south):
        pl.semaphore_signal(barrier, inc=1, device_id={"lat": place}, device_id_type=MESH)
    for offset in range(1, n_lev):
        pl.semaphore_signal(barrier, inc=1, device_id={"lev": lax.rem(lev + offset, n_lev)}, device_id_type=MESH)
    load = pltpu.make_async_copy(tables_in, tables, table_sem)

    @pl.when(polar)
    def _():
        load.start()

    arrays = (thick_in, tracer_in, lat_in, lon_in)
    for which, array in enumerate(arrays):
        for level in range(levels):
            for side, first in ((0, rows - 2), (1, 0)):
                for row in range(2):
                    pack[side, which, pl.ds(row * levels + level, 1), :] = array[level, pl.ds(first + row, 1), :]
    pl.semaphore_wait(barrier, n_lev + 1)
    copies = []
    for side, place in ((0, north), (1, south)):
        copy = pltpu.make_async_remote_copy(
            src_ref=pack.at[side], dst_ref=halo.at[side], send_sem=halo_sent.at[side], recv_sem=halo_got.at[side],
            device_id={"lat": place}, device_id_type=MESH,
        )
        copy.start()
        copies.append(copy)
    for copy in copies:
        copy.wait()

    first_row = lat * rows
    def around(which):
        below, above = halo[0, which], halo[1, which]
        mine_last, mine_first = pack[0, which], pack[1, which]
        before = jnp.concatenate([below[:levels], mine_last[levels:]], axis=0)
        here = jnp.concatenate([below[levels:], above[:levels]], axis=0)
        after = jnp.concatenate([mine_first[:levels], above[levels:]], axis=0)
        return before, here, after

    sub = lax.broadcasted_iota(jnp.int32, (2 * levels, 1), 0)
    edge_row = jnp.where(sub < levels, first_row - 1, first_row + rows)
    lat_before, lat_here, lat_after = around(2)
    below_lon, above_lon = halo[0, 3], halo[1, 3]
    lon_here = jnp.concatenate([below_lon[levels:], above_lon[:levels]], axis=0)
    edge_south = 0.5 * (lat_before + lat_here)
    edge_north = 0.5 * (lat_here + lat_after)
    cos_south = face_cosine(edge_row - 1, lat_total)
    cos_north = face_cosine(edge_row, lat_total)
    edge_inv = 1.0 / cell_cosine(edge_row, lat_total)
    south_pos, south_neg = jnp.maximum(edge_south, 0.0) * cos_south, jnp.minimum(edge_south, 0.0) * cos_south
    north_pos, north_neg = jnp.maximum(edge_north, 0.0) * cos_north, jnp.minimum(edge_north, 0.0) * cos_north
    lon_pos, lon_neg = jnp.maximum(lon_here, 0.0), jnp.minimum(lon_here, 0.0)
    for which in range(2):
        before, here, after = around(which)
        edge_first[which] = advance(
            here, after, lambda _: south_pos * before + south_neg * here,
            lon_pos, lon_neg, north_pos, north_neg, edge_inv,
        )
    row_index = first_row + lax.broadcasted_iota(jnp.int32, (rows, 1), 0)
    cos_faces = face_cosine(row_index, lat_total)
    inv_cos = 1.0 / cell_cosine(row_index, lat_total)
    cos_first = face_cosine(jnp.full((1, 1), first_row - 1, jnp.int32), lat_total)

    @pl.loop(0, levels)
    def _(level):
        lat_now = lat_in[level]
        below_lat = halo[0, 2, pl.ds(levels + level, 1), :]
        above_lat = halo[1, 2, pl.ds(level, 1), :]
        a_north = 0.5 * (lat_now + jnp.concatenate([lat_now[1:], above_lat], axis=0))
        a_first = 0.5 * (below_lat + lat_now[:1])
        lat_pos, lat_neg = jnp.maximum(a_north, 0.0) * cos_faces, jnp.minimum(a_north, 0.0) * cos_faces
        first_pos, first_neg = jnp.maximum(a_first, 0.0) * cos_first, jnp.minimum(a_first, 0.0) * cos_first
        lon_now = lon_in[level]
        lon_pos, lon_neg = jnp.maximum(lon_now, 0.0), jnp.minimum(lon_now, 0.0)
        for which, array in enumerate((thick_in, tracer_in)):
            start = array[level]
            field = start
            for step in range(ITERS):
                if step == 0:
                    low = halo[0, which, pl.ds(levels + level, 1), :]
                    high = halo[1, which, pl.ds(level, 1), :]
                else:
                    low = edge_first[which, pl.ds(level, 1), :]
                    high = edge_first[which, pl.ds(levels + level, 1), :]
                first_flux = first_pos * low + first_neg * field[:1]
                field = advance(
                    field, jnp.concatenate([field[1:], high], axis=0),
                    lambda flux: jnp.concatenate([first_flux, flux[:-1]], axis=0),
                    lon_pos, lon_neg, lat_pos, lat_neg, inv_cos,
                )
            place = pl.ds(pl.multiple_of(level * rows, rows), rows)
            if which == 0:
                thick_rows[place, :] = field
            else:
                tend = field - start
                tend_rows[place, :] = tend
                tracer_rows[place, :] = start + tend

    def to_columns(source, target):
        for block in range(width // LANES):
            piece = pl.ds(block * LANES, LANES)
            target[piece, :] = source[:, piece].T

    def send(source, target, sent, got):
        started = []
        for offset in range(1, n_lev):
            other = lax.rem(lev + offset, n_lev)
            copy = pltpu.make_async_remote_copy(
                src_ref=source.at[pl.ds(pl.multiple_of(other * dest, 8), dest)], dst_ref=target.at[lev],
                send_sem=sent.at[offset - 1], recv_sem=got.at[offset - 1], device_id={"lev": other}, device_id_type=MESH,
            )
            copy.start()
            started.append(copy)
        return started

    to_columns(thick_rows, thick_send)
    started = send(thick_send, thick_out, thick_sent, thick_got)
    to_columns(tracer_rows, tracer_send)

    @pl.when(polar)
    def _():
        to_columns(tend_rows, tend_cols)
        half = width // 2
        quarter = half // 2
        for level in range(levels):
            cut_lanes[:, pl.ds(level * rows, rows)] = jnp.broadcast_to(cut_in[...].astype(jnp.float32), (8, rows))
        cut = cut_lanes[pl.ds(0, 1), :]
        load.wait()
        index = lax.broadcasted_iota(jnp.int32, (half, 1), 0)
        first, second = tend_cols[pl.ds(0, half), :], tend_cols[pl.ds(half, half), :]

        def times(stage, parity, columns):
            high = columns.astype(jnp.bfloat16)
            low = (columns - high.astype(jnp.float32)).astype(jnp.bfloat16)
            both = jnp.dot(tables[2 * stage, parity], jnp.concatenate([high, low], axis=1), preferred_element_type=jnp.float32)
            rest = jnp.dot(tables[2 * stage + 1, parity], high, preferred_element_type=jnp.float32)
            return both[:, :LANES] + (both[:, LANES:] + rest)

        changes = []
        for parity in range(2):
            if parity == 0:
                wave = jnp.where(index <= quarter, 2 * index, 2 * (index - quarter))
            else:
                wave = jnp.where(index < quarter, 2 * index + 1, 2 * (index - quarter) + 1)
            ratio = cut * (1.0 / jnp.maximum(wave, 1).astype(jnp.float32))
            damping = jnp.where(wave == 0, 1.0, jnp.minimum(1.0, ratio * ratio))
            coefficients = times(0, parity, first + second if parity == 0 else first - second)
            changes.append(times(1, parity, coefficients * (damping - 1.0)))
        tracer_send[pl.ds(0, half), :] += changes[0] + changes[1]
        tracer_send[pl.ds(half, half), :] += changes[0] - changes[1]

    moved = send(tracer_send, tracer_out, tracer_sent, tracer_got)
    mine = pl.ds(pl.multiple_of(lev * dest, 8), dest)
    thick_out[lev] = thick_send[mine, :]
    tracer_out[lev] = tracer_send[mine, :]
    for copy in started + moved:
        copy.wait()


def remap_kernel(thick, tracer, weights, new_thick, new_tracer, fraction, fraction_cols, tops_turned, slopes_turned, below, mass_cols):
    sources, dest, _ = thick.shape
    level_total, rows, _ = weights.shape
    levels = LANES // rows
    groups = level_total // levels
    total = jnp.zeros((rows, dest), jnp.int32)
    for level in range(level_total):
        total = total + weights[level]
        fraction[level, :, pl.ds(0, dest)] = total.astype(jnp.float32)
    inverse = 1.0 / total.astype(jnp.float32)
    for level in range(level_total):
        fraction[level, :, pl.ds(0, dest)] = fraction[level, :, pl.ds(0, dest)] * inverse
    for group in range(groups):
        block = fraction[pl.ds(group * levels, levels)].reshape(LANES, LANES)
        fraction_cols[group] = block.T[:dest]
    lane_level = lax.broadcasted_iota(jnp.int32, (8, LANES), 1) // rows

    def turn(values, count):
        return pltpu.roll(values, count * rows, axis=1)

    @pl.loop(0, dest // 8)
    def _(piece):
        here = pl.ds(pl.multiple_of(piece * 8, 8), 8)
        carry = jnp.zeros((8, LANES), jnp.float32)
        offset = jnp.zeros((8, LANES), jnp.float32)
        last = jnp.zeros((8, LANES), jnp.float32)
        for source in range(sources):
            layer = thick[source, here, :]
            ratio = tracer[source, here, :] / layer
            one = turn(layer, 1)
            two = layer + jnp.where(lane_level >= 1, one, 0.0)
            inclusive = two + jnp.where(lane_level >= 2, turn(two, 2), 0.0)
            pair = layer + one
            tops = carry + (inclusive - layer)
            carry = carry + (pair + turn(pair, 2))
            moved = turn(ratio, 1)
            slope = ratio - jnp.where(lane_level >= 1, moved, last)
            last = moved
            offset = offset + slope * tops
            for count in range(levels):
                tops_turned[source * levels + count] = turn(tops, count) if count else tops
                slopes_turned[source * levels + count] = turn(slope, count) if count else slope
        offset = offset + turn(offset, 1)
        offset = offset + turn(offset, 2)
        mass_cols[here, :] = carry
        targets = [carry * fraction_cols[group, here, :] for group in range(groups)]

        def accumulate(index, sums):
            tops, slope = tops_turned[index], slopes_turned[index]
            return tuple(s + slope * jnp.maximum(t, tops) for s, t in zip(sums, targets))

        sums = lax.fori_loop(0, sources * levels, accumulate, (jnp.zeros((8, LANES), jnp.float32),) * groups, unroll=4)
        for group in range(groups):
            below[group, here, :] = sums[group] - offset

    mass = mass_cols[...].T[:rows, :dest]
    before = jnp.zeros((levels, rows, dest), jnp.float32)
    target_before = jnp.zeros((rows, dest), jnp.float32)
    below_before = jnp.zeros((rows, dest), jnp.float32)
    for group in range(groups):
        block = below[group].T.reshape(levels, rows, LANES)
        for inner in range(levels):
            level = group * levels + inner
            target = mass * fraction[level, :, pl.ds(0, dest)]
            new_thick[level] = target - target_before
            target_before = target
            now = block[inner, :, :dest]
            new_tracer[level] = now - below_before
            below_before = now


def on_device(n_lat, n_lev, thickness, tracer_mass, courant_lon, courant_lat, filter_cut, target_weights):
    levels, rows, width = thickness.shape
    lat_total = n_lat * rows
    dest = width // n_lev
    half = width // 2
    tables = fourier_tables(width)
    vmem = pl.BlockSpec(memory_space=pltpu.VMEM)
    columns = jax.ShapeDtypeStruct((n_lev, dest, LANES), jnp.float32)
    f32 = jnp.float32
    dma = pltpu.SemaphoreType.DMA
    thick_cols, tracer_cols = pl.pallas_call(
        functools.partial(move_kernel, n_lat, n_lev, lat_total),
        out_shape=(columns, columns),
        in_specs=[vmem] * 5 + [pl.BlockSpec(memory_space=pl.ANY)],
        out_specs=(vmem, vmem),
        scratch_shapes=[
            pltpu.VMEM((2, 4, 2 * levels, width), f32),
            pltpu.VMEM((2, 4, 2 * levels, width), f32),
            pltpu.VMEM((2, 2 * levels, width), f32),
            pltpu.VMEM((LANES, width), f32),
            pltpu.VMEM((LANES, width), f32),
            pltpu.VMEM((LANES, width), f32),
            pltpu.VMEM((width, LANES), f32),
            pltpu.VMEM((width, LANES), f32),
            pltpu.VMEM((width, LANES), f32),
            pltpu.VMEM((8, LANES), f32),
            pltpu.VMEM(tables.shape, jnp.bfloat16),
            dma((2,)), dma((2,)), *[dma((n_lev - 1,))] * 4, dma,
        ],
        compiler_params=pltpu.CompilerParams(collective_id=0, has_side_effects=True, vmem_limit_bytes=48 << 20),
        name="move",
    )(thickness, tracer_mass, courant_lon, courant_lat, filter_cut.reshape(1, rows), jnp.asarray(tables))
    level_total = target_weights.shape[0]
    groups = level_total * rows // LANES
    result = jax.ShapeDtypeStruct(target_weights.shape, f32)
    return pl.pallas_call(
        remap_kernel,
        out_shape=(result, result),
        in_specs=[vmem] * 3,
        out_specs=(vmem, vmem),
        scratch_shapes=[
            pltpu.VMEM((level_total, rows, LANES), f32),
            pltpu.VMEM((groups, dest, LANES), f32),
            pltpu.VMEM((level_total, 8, LANES), f32),
            pltpu.VMEM((level_total, 8, LANES), f32),
            pltpu.VMEM((groups, LANES, LANES), f32),
            pltpu.VMEM((LANES, LANES), f32),
        ],
        compiler_params=pltpu.CompilerParams(vmem_limit_bytes=48 << 20),
        name="remap",
    )(thick_cols, tracer_cols, target_weights)


def solution(mesh):
    n_lat, n_lev = mesh.shape["lat"], mesh.shape["lev"]
    placed = (
        P("lev", "lat", None),
        P("lev", "lat", None),
        P("lev", "lat", None),
        P("lev", "lat", None),
        P("lat"),
        P(None, "lat", "lev"),
    )
    return jax.shard_map(
        functools.partial(on_device, n_lat, n_lev),
        mesh=mesh,
        in_specs=placed,
        out_specs=(P(None, "lat", "lev"), P(None, "lat", "lev")),
        check_vma=False,
    )
```

```python
import functools

import jax
import jax.numpy as jnp
import ml_dtypes
import numpy as np
from jax import lax
from jax.experimental import pallas as pl
from jax.experimental.pallas import tpu as pltpu
from jax.sharding import PartitionSpec as P

ITERS = 2
LANES = 128
MESH = pl.DeviceIdType.MESH


def split_bf16(table):
    high = table.astype(ml_dtypes.bfloat16)
    low = (table - high.astype(np.float64)).astype(ml_dtypes.bfloat16)
    return high, low


def fourier_tables(lon):
    half = lon // 2
    quarter = half // 2
    index = np.arange(half)
    even_wave = np.where(index <= quarter, 2 * index, 2 * (index - quarter))
    even_sine = index > quarter
    odd_wave = np.where(index < quarter, 2 * index + 1, 2 * (index - quarter) + 1)
    odd_sine = index >= quarter
    parts = []
    inverse = []
    for wave, sine in ((even_wave, even_sine), (odd_wave, odd_sine)):
        phase = 2.0 * np.pi / lon * (wave[:, None] * index[None, :] % lon)
        basis = np.where(sine[:, None], np.sin(phase), np.cos(phase))
        scale = np.where((wave == 0) | (wave == half), 1.0 / lon, 2.0 / lon)
        parts.append(basis)
        inverse.append((basis * scale[:, None]).T)
    forward_high, forward_low = split_bf16(np.stack(parts))
    inverse_high, inverse_low = split_bf16(np.stack(inverse))
    return np.stack([forward_high, forward_low, inverse_high, inverse_low])


def face_cosine(row, lat_total):
    return jnp.sin(jnp.pi / lat_total * jnp.minimum(row + 1, lat_total - row - 1).astype(jnp.float32))


def cell_cosine(row, lat_total):
    return jnp.sin(jnp.pi / lat_total * (row.astype(jnp.float32) + 0.5))


def advance(field, north, south_flux, lon_pos, lon_neg, lat_pos, lat_neg, inv_cos):
    width = field.shape[1]
    east = pltpu.roll(field, width - 1, axis=1)
    lon_flux = lon_pos * field + lon_neg * east
    lat_flux = lat_pos * field + lat_neg * north
    return field - (lon_flux - pltpu.roll(lon_flux, 1, axis=1)) - (lat_flux - south_flux(lat_flux)) * inv_cos


def by_sign(courant, scale=None):
    parts = jnp.maximum(courant, 0.0), jnp.minimum(courant, 0.0)
    return parts if scale is None else tuple(part * scale for part in parts)


def transport(lat, lat_total, arrays, pack, extra, inner_first, halo, exchange, thick_rows, tracer_rows, tend_rows):
    levels, rows, width = arrays[0].shape
    first_row = lat * rows
    for which, array in enumerate(arrays):
        for level in range(levels):
            for row in range(2):
                pack[0, which, pl.ds(row * levels + level, 1), :] = array[level, pl.ds(rows - 2 + row, 1), :]
                pack[1, which, pl.ds(row * levels + level, 1), :] = array[level, pl.ds(row, 1), :]
                extra[which, pl.ds(row * levels + level, 1), :] = array[level, pl.ds((2, rows - 3)[row], 1), :]
    finish = exchange()
    thick, tracer, lat_courant, lon_courant = arrays
    row_index = first_row + lax.broadcasted_iota(jnp.int32, (rows, 1), 0)
    cos_faces = face_cosine(row_index, lat_total)
    inv_cos = 1.0 / cell_cosine(row_index, lat_total)

    @pl.loop(0, levels)
    def _(level):
        lat_now = lat_courant[level]
        lat_pos, lat_neg = by_sign(0.5 * (lat_now + pltpu.roll(lat_now, rows - 1, axis=0)), cos_faces)
        lon_pos, lon_neg = by_sign(lon_courant[level])
        place = pl.ds(pl.multiple_of(level * rows, rows), rows)
        for which, array in enumerate((thick, tracer)):
            start = array[level]
            field = start
            for step in range(ITERS):
                field = advance(
                    field, pltpu.roll(field, rows - 1, axis=0), lambda flux: pltpu.roll(flux, 1, axis=0),
                    lon_pos, lon_neg, lat_pos, lat_neg, inv_cos,
                )
                if step == 0:
                    inner_first[which, pl.ds(level, 1), :] = field[2:3]
                    inner_first[which, pl.ds(levels + level, 1), :] = field[rows - 3 : rows - 2]
            if which == 0:
                thick_rows[place, :] = field
            else:
                tend = field - start
                tend_rows[place, :] = tend
                tracer_rows[place, :] = start + tend

    finish()
    sub = lax.broadcasted_iota(jnp.int32, (2 * levels, 1), 0)
    strip_row = jnp.where(sub < levels, first_row - 2, first_row + rows - 3)
    cos_strip = [face_cosine(strip_row + p, lat_total) for p in range(4)]
    inv_strip = [1.0 / cell_cosine(strip_row + p, lat_total) for p in range(4)]

    def strip(which):
        below, above = halo[0, which], halo[1, which]
        last, first, third = pack[0, which], pack[1, which], extra[which]
        halves = (
            (below[:levels], third[levels:]),
            (below[levels:], last[:levels]),
            (first[:levels], last[levels:]),
            (first[levels:], above[:levels]),
            (third[:levels], above[levels:]),
        )
        return [jnp.concatenate(pair, axis=0) for pair in halves]

    lat_strip = strip(2)
    lat_parts = [by_sign(0.5 * (lat_strip[p] + lat_strip[p + 1]), cos_strip[p]) for p in range(4)]
    lon_parts = [by_sign(values) for values in strip(3)]
    for which in range(2):
        start = strip(which)
        field = start
        for step in range(ITERS):
            moved = []
            flux = lat_parts[0][0] * field[0] + lat_parts[0][1] * field[1]
            for p in range(1, 4):
                before = flux
                moved.append(advance(
                    field[p], field[p + 1], lambda _: before,
                    *lon_parts[p], *lat_parts[p], inv_strip[p],
                ))
                flux = lat_parts[p][0] * field[p] + lat_parts[p][1] * field[p + 1]
            field = [inner_first[which], *moved, inner_first[which]]
        for p, side, row in ((2, 0, 0), (3, 0, 1), (1, 1, rows - 2), (2, 1, rows - 1)):
            tend = field[p] - start[p]
            done = start[p] + tend
            for level in range(levels):
                source = slice(side * levels + level, side * levels + level + 1)
                place = pl.ds(level * rows + row, 1)
                if which == 0:
                    thick_rows[place, :] = field[p][source]
                else:
                    tend_rows[place, :] = tend[source]
                    tracer_rows[place, :] = done[source]


def to_columns(source, target):
    for block in range(source.shape[1] // LANES):
        piece = pl.ds(block * LANES, LANES)
        target[piece, :] = source[:, piece].T


def add_damped(cut, tend, tables, tracer):
    half = tend.shape[0] // 2
    quarter = half // 2
    index = lax.broadcasted_iota(jnp.int32, (half, 1), 0)
    first, second = tend[pl.ds(0, half), :], tend[pl.ds(half, half), :]

    def times(stage, parity, columns):
        high = columns.astype(jnp.bfloat16)
        low = (columns - high.astype(jnp.float32)).astype(jnp.bfloat16)
        both = jnp.dot(tables[2 * stage, parity], jnp.concatenate([high, low], axis=1), preferred_element_type=jnp.float32)
        rest = jnp.dot(tables[2 * stage + 1, parity], high, preferred_element_type=jnp.float32)
        return both[:, :LANES] + (both[:, LANES:] + rest)

    changes = []
    for parity in range(2):
        if parity == 0:
            wave = jnp.where(index <= quarter, 2 * index, 2 * (index - quarter))
        else:
            wave = jnp.where(index < quarter, 2 * index + 1, 2 * (index - quarter) + 1)
        ratio = cut * (1.0 / jnp.maximum(wave, 1).astype(jnp.float32))
        damping = jnp.where(wave == 0, 1.0, jnp.minimum(1.0, ratio * ratio))
        coefficients = times(0, parity, first + second if parity == 0 else first - second)
        changes.append(times(1, parity, coefficients * (damping - 1.0)))
    tracer[pl.ds(0, half), :] += changes[0] + changes[1]
    tracer[pl.ds(half, half), :] += changes[0] - changes[1]


def prepare_weights(weights, fraction, fraction_cols):
    level_total, rows, dest = weights.shape
    levels = LANES // rows

    def add(level, total):
        total = total + weights[level]
        fraction[level, :, pl.ds(0, dest)] = total.astype(jnp.float32)
        return total

    total = lax.fori_loop(0, level_total, add, jnp.zeros((rows, dest), jnp.int32), unroll=8)
    inverse = 1.0 / total.astype(jnp.float32)

    @pl.loop(0, level_total // levels)
    def _(group):
        here = pl.ds(group * levels, levels)
        scaled = fraction[here, :, pl.ds(0, dest)] * inverse[None]
        fraction[here, :, pl.ds(0, dest)] = scaled
        fraction_cols[group] = fraction[here].reshape(LANES, LANES).T[:dest]


def interpolate(rows, piece, thick, tracer, fraction_cols, tops_turned, slopes_turned, below, mass_cols):
    sources = thick.shape[0]
    levels = LANES // rows
    groups = sources
    lane_level = lax.broadcasted_iota(jnp.int32, (8, LANES), 1) // rows
    here = pl.ds(pl.multiple_of(piece * 8, 8), 8)
    zero = jnp.zeros((8, LANES), jnp.float32)

    def turn(values, count):
        return pltpu.roll(values, count * rows, axis=1)

    carry = offset = last = zero
    for source in range(sources):
        layer = thick[source, here, :]
        ratio = tracer[source, here, :] / layer
        one = turn(layer, 1)
        two = layer + jnp.where(lane_level >= 1, one, 0.0)
        inclusive = two + jnp.where(lane_level >= 2, turn(two, 2), 0.0)
        pair = layer + one
        tops = carry + (inclusive - layer)
        carry = carry + (pair + turn(pair, 2))
        moved = turn(ratio, 1)
        slope = ratio - jnp.where(lane_level >= 1, moved, last)
        last = moved
        offset = offset + slope * tops
        for count in range(levels):
            tops_turned[source * levels + count] = turn(tops, count) if count else tops
            slopes_turned[source * levels + count] = turn(slope, count) if count else slope
    offset = offset + turn(offset, 1)
    offset = offset + turn(offset, 2)
    mass_cols[here, :] = carry
    targets = [carry * fraction_cols[group, here, :] for group in range(groups)]

    def accumulate(index, sums):
        tops, slope = tops_turned[index], slopes_turned[index]
        return tuple(s + slope * jnp.maximum(t, tops) for s, t in zip(sums, targets))

    sums = lax.fori_loop(0, sources * levels, accumulate, (zero,) * groups, unroll=4)
    for group in range(groups):
        below[group, here, :] = sums[group] - offset


def step_kernel(
    n_lat, n_lev, lat_total, chunks,
    thick_hbm, tracer_hbm, lon_hbm, lat_hbm, cut_hbm, weights_hbm, tables_hbm,
    below, fraction, mass_cols,
    thick_in, tracer_in, lon_in, lat_in, cut_in, weights_in, tables,
    pack, halo, extra, inner_first, thick_rows, tracer_rows, tend_rows, thick_send, tracer_send, tend_cols, cut_lanes,
    thick_cols, tracer_cols, fraction_cols, tops_turned, slopes_turned,
    load_sem, halo_sent, halo_got, sent, got,
):
    levels, rows, width = thick_in.shape
    dest = width // n_lev
    lat = lax.axis_index("lat")
    lev = lax.axis_index("lev")
    north = lax.rem(lat + 1, n_lat)
    south = lax.rem(lat + n_lat - 1, n_lat)
    polar = (lat < 2) | (lat >= n_lat - 2)
    barrier = pltpu.get_barrier_semaphore()
    for place in (north, south):
        pl.semaphore_signal(barrier, inc=1, device_id={"lat": place}, device_id_type=MESH)
    for offset in range(1, n_lev):
        pl.semaphore_signal(barrier, inc=1, device_id={"lev": lax.rem(lev + offset, n_lev)}, device_id_type=MESH)
    pairs = (
        (thick_hbm, thick_in), (tracer_hbm, tracer_in), (lat_hbm, lat_in), (lon_hbm, lon_in),
        (weights_hbm, weights_in), (cut_hbm, cut_in), (tables_hbm, tables),
    )
    loads = [pltpu.make_async_copy(source, target, load_sem.at[i]) for i, (source, target) in enumerate(pairs)]
    for load in loads[:6]:
        load.start()

    @pl.when(polar)
    def _():
        loads[6].start()

    for load in loads[:4]:
        load.wait()

    def exchange():
        pl.semaphore_wait(barrier, n_lev + 1)
        copies = []
        for side, place in ((0, north), (1, south)):
            copy = pltpu.make_async_remote_copy(
                src_ref=pack.at[side], dst_ref=halo.at[side], send_sem=halo_sent.at[side], recv_sem=halo_got.at[side],
                device_id={"lat": place}, device_id_type=MESH,
            )
            copy.start()
            copies.append(copy)

        def finish():
            for copy in copies:
                copy.wait()

        return finish

    transport(
        lat, lat_total, (thick_in, tracer_in, lat_in, lon_in), pack, extra, inner_first, halo, exchange,
        thick_rows, tracer_rows, tend_rows,
    )

    def send(source, target, which, first, count):
        started = []
        for offset in range(1, n_lev):
            other = lax.rem(lev + offset, n_lev)
            copy = pltpu.make_async_remote_copy(
                src_ref=source.at[pl.ds(pl.multiple_of(other * dest + first, 8), count)],
                dst_ref=target.at[lev, pl.ds(first, count)],
                send_sem=sent.at[which, offset - 1], recv_sem=got.at[which, offset - 1],
                device_id={"lev": other}, device_id_type=MESH,
            )
            copy.start()
            started.append(copy)
        return started

    to_columns(thick_rows, thick_send)
    thick_copies = send(thick_send, thick_cols, 0, 0, dest)
    to_columns(tracer_rows, tracer_send)
    for load in loads[4:6]:
        load.wait()

    @pl.when(polar)
    def _():
        to_columns(tend_rows, tend_cols)
        for level in range(levels):
            cut_lanes[:, pl.ds(level * rows, rows)] = jnp.broadcast_to(cut_in[...].astype(jnp.float32), (8, rows))
        loads[6].wait()
        add_damped(cut_lanes[pl.ds(0, 1), :], tend_cols, tables, tracer_send)

    bounds = [sum(chunks[:i]) for i in range(len(chunks) + 1)]
    tracer_copies = [
        send(tracer_send, tracer_cols, 1 + i, 8 * bounds[i], 8 * chunks[i]) for i in range(len(chunks))
    ]
    mine = pl.ds(pl.multiple_of(lev * dest, 8), dest)
    thick_cols[lev] = thick_send[mine, :]
    tracer_cols[lev] = tracer_send[mine, :]
    prepare_weights(weights_in, fraction, fraction_cols)
    for copy in thick_copies:
        copy.wait()
    for i in range(len(chunks)):
        for copy in tracer_copies[i]:
            copy.wait()

        @pl.loop(bounds[i], bounds[i + 1])
        def _(piece):
            interpolate(rows, piece, thick_cols, tracer_cols, fraction_cols, tops_turned, slopes_turned, below, mass_cols)


def finish_kernel(below, fraction, mass_cols, thick_hbm, tracer_hbm, new_thick, new_tracer, sems):
    groups = below.shape[0]
    levels, rows, dest = new_thick.shape[0] // groups, new_thick.shape[1], new_thick.shape[2]
    mass = mass_cols[...].T[:rows, :dest]
    target_before = below_before = jnp.zeros((rows, dest), jnp.float32)
    copies = []

    def put(which, group, source, target):
        place = pl.ds(group * levels, levels)
        copy = pltpu.make_async_copy(source.at[place], target.at[place], sems.at[which, group])
        copy.start()
        copies.append(copy)

    for group in range(groups):
        block = below[group].T.reshape(levels, rows, LANES)
        for inner in range(levels):
            level = group * levels + inner
            target = mass * fraction[level, :, pl.ds(0, dest)]
            new_thick[level] = target - target_before
            target_before = target
            now = block[inner, :, :dest]
            new_tracer[level] = now - below_before
            below_before = now
        put(0, group, new_thick, thick_hbm)
        put(1, group, new_tracer, tracer_hbm)
    for copy in copies:
        copy.wait()


def chunks_of(pieces):
    half = (pieces - 1) // 2
    return (pieces - 1 - half, half, 1)


def on_device(n_lat, n_lev, thickness, tracer_mass, courant_lon, courant_lat, filter_cut, target_weights):
    levels, rows, width = thickness.shape
    lat_total = n_lat * rows
    dest = width // n_lev
    level_total = target_weights.shape[0]
    groups = level_total * rows // LANES
    tables = fourier_tables(width)
    chunks = chunks_of(dest // 8)
    vmem, hbm = pl.BlockSpec(memory_space=pltpu.VMEM), pl.BlockSpec(memory_space=pltpu.HBM)
    f32, dma = jnp.float32, pltpu.SemaphoreType.DMA
    block = thickness.shape
    sums = (
        jax.ShapeDtypeStruct((groups, LANES, LANES), f32),
        jax.ShapeDtypeStruct((level_total, rows, LANES), f32),
        jax.ShapeDtypeStruct((LANES, LANES), f32),
    )
    shapes = (
        *[block] * 4, (1, rows), target_weights.shape, tables.shape,
        (2, 4, 2 * levels, width), (2, 4, 2 * levels, width), (4, 2 * levels, width), (2, 2 * levels, width),
        *[(LANES, width)] * 3, *[(width, LANES)] * 3, (8, LANES),
        (n_lev, dest, LANES), (n_lev, dest, LANES), (groups, dest, LANES), (level_total, 8, LANES), (level_total, 8, LANES),
    )
    kinds = [f32] * 4 + [jnp.int32] * 2 + [jnp.bfloat16] + [f32] * (len(shapes) - 7)
    arrays = (
        thickness, tracer_mass, courant_lon, courant_lat, filter_cut.reshape(1, rows), target_weights, jnp.asarray(tables),
    )
    columns = pl.pallas_call(
        functools.partial(step_kernel, n_lat, n_lev, lat_total, chunks),
        out_shape=sums,
        in_specs=[hbm] * 7,
        out_specs=(vmem,) * 3,
        scratch_shapes=[pltpu.VMEM(shape, kind) for shape, kind in zip(shapes, kinds)]
        + [dma((7,)), dma((2,)), dma((2,)), dma((1 + len(chunks), n_lev - 1)), dma((1 + len(chunks), n_lev - 1))],
        compiler_params=pltpu.CompilerParams(collective_id=0, has_side_effects=True, vmem_limit_bytes=48 << 20),
        name="step",
    )(*(pltpu.with_memory_space_constraint(array, pltpu.HBM) for array in arrays))
    result = jax.ShapeDtypeStruct(target_weights.shape, f32)
    return pl.pallas_call(
        finish_kernel,
        out_shape=(result, result),
        in_specs=[vmem] * 3,
        out_specs=(hbm, hbm),
        scratch_shapes=[
            pltpu.VMEM(target_weights.shape, f32), pltpu.VMEM(target_weights.shape, f32), dma((2, groups)),
        ],
        compiler_params=pltpu.CompilerParams(vmem_limit_bytes=32 << 20),
        name="finish",
    )(*columns)


def solution(mesh):
    n_lat, n_lev = mesh.shape["lat"], mesh.shape["lev"]
    placed = (
        P("lev", "lat", None),
        P("lev", "lat", None),
        P("lev", "lat", None),
        P("lev", "lat", None),
        P("lat"),
        P(None, "lat", "lev"),
    )
    return jax.shard_map(
        functools.partial(on_device, n_lat, n_lev),
        mesh=mesh,
        in_specs=placed,
        out_specs=(P(None, "lat", "lev"), P(None, "lat", "lev")),
        check_vma=False,
    )
```

```python
import functools

import jax
import jax.numpy as jnp
import ml_dtypes
import numpy as np
from jax import lax
from jax.experimental import pallas as pl
from jax.experimental.pallas import tpu as pltpu
from jax.sharding import PartitionSpec as P

ITERS = 2
LANES = 128
MESH = pl.DeviceIdType.MESH


def split_bf16(table):
    high = table.astype(ml_dtypes.bfloat16)
    low = (table - high.astype(np.float64)).astype(ml_dtypes.bfloat16)
    return high, low


def fourier_tables(lon):
    half = lon // 2
    quarter = half // 2
    index = np.arange(half)
    even_wave = np.where(index <= quarter, 2 * index, 2 * (index - quarter))
    even_sine = index > quarter
    odd_wave = np.where(index < quarter, 2 * index + 1, 2 * (index - quarter) + 1)
    odd_sine = index >= quarter
    parts = []
    inverse = []
    for wave, sine in ((even_wave, even_sine), (odd_wave, odd_sine)):
        phase = 2.0 * np.pi / lon * (wave[:, None] * index[None, :] % lon)
        basis = np.where(sine[:, None], np.sin(phase), np.cos(phase))
        scale = np.where((wave == 0) | (wave == half), 1.0 / lon, 2.0 / lon)
        parts.append(basis)
        inverse.append((basis * scale[:, None]).T)
    forward_high, forward_low = split_bf16(np.stack(parts))
    inverse_high, inverse_low = split_bf16(np.stack(inverse))
    return np.stack([forward_high, forward_low, inverse_high, inverse_low])


def face_cosine(row, lat_total):
    return jnp.sin(jnp.pi / lat_total * jnp.minimum(row + 1, lat_total - row - 1).astype(jnp.float32))


def cell_cosine(row, lat_total):
    return jnp.sin(jnp.pi / lat_total * (row.astype(jnp.float32) + 0.5))


def advance(field, north, south_flux, lon_pos, lon_neg, lat_pos, lat_neg, inv_cos):
    width = field.shape[1]
    east = pltpu.roll(field, width - 1, axis=1)
    lon_flux = lon_pos * field + lon_neg * east
    lat_flux = lat_pos * field + lat_neg * north
    return field - (lon_flux - pltpu.roll(lon_flux, 1, axis=1)) - (lat_flux - south_flux(lat_flux)) * inv_cos


def by_sign(courant, scale=None):
    parts = jnp.maximum(courant, 0.0), jnp.minimum(courant, 0.0)
    return parts if scale is None else tuple(part * scale for part in parts)


def spread(rows):
    return jnp.concatenate([rows[..., 8:, :], rows[..., :8, :]], axis=-2)


def lane_half(rows):
    return lax.rem(lax.broadcasted_iota(jnp.int32, (8, LANES), 1), rows) < rows // 2


def pair_up(first, second, rows):
    low = lane_half(rows)
    middle = jnp.where(low, first, pltpu.roll(second, rows // 2, axis=1))
    outer = jnp.where(low, pltpu.roll(first, LANES - rows // 2, axis=1), second)
    return middle, outer


def inner_rows(lat_total, arrays, arrive, thick_rows, tracer_rows, tend_rows, to_north, to_south, third, inner_first):
    thick, tracer, lat_courant, lon_courant = arrays
    levels, rows, width = thick.shape
    first_row = lax.axis_index("lat") * rows
    row_index = first_row + lax.broadcasted_iota(jnp.int32, (rows, 1), 0)
    cos_faces = face_cosine(row_index, lat_total)
    inv_cos = 1.0 / cell_cosine(row_index, lat_total)

    @pl.loop(0, levels)
    def _(level):
        arrive(level)
        for which, array in enumerate(arrays):
            for row in range(2):
                place = pl.ds(row * levels + level, 1)
                to_north[which, place, :] = array[level, pl.ds(rows - 2 + row, 1), :]
                to_south[which, place, :] = array[level, pl.ds(row, 1), :]
                third[which, place, :] = array[level, pl.ds((2, rows - 3)[row], 1), :]
        lat_now = lat_courant[level]
        lat_pos, lat_neg = by_sign(0.5 * (lat_now + pltpu.roll(lat_now, rows - 1, axis=0)), cos_faces)
        lon_pos, lon_neg = by_sign(lon_courant[level])
        place = pl.ds(pl.multiple_of(level * rows, rows), rows)
        for which, array in enumerate((thick, tracer)):
            start = array[level]
            field = start
            for step in range(ITERS):
                field = advance(
                    field, pltpu.roll(field, rows - 1, axis=0), lambda flux: pltpu.roll(flux, 1, axis=0),
                    lon_pos, lon_neg, lat_pos, lat_neg, inv_cos,
                )
                if step == 0:
                    inner_first[which, pl.ds(level, 1), :] = field[2:3]
                    inner_first[which, pl.ds(levels + level, 1), :] = field[rows - 3 : rows - 2]
            if which == 0:
                thick_rows[place, :] = spread(field)
            else:
                tend = field - start
                tend_rows[place, :] = spread(tend)
                tracer_rows[place, :] = spread(start + tend)


def edges(lat_total, rows, below, above, to_north, to_south, third, inner_first, thick_rows, tracer_rows, tend_rows):
    levels = below.shape[1] // 2
    first_row = lax.axis_index("lat") * rows
    sub = lax.broadcasted_iota(jnp.int32, (2 * levels, 1), 0)
    strip_row = jnp.where(sub < levels, first_row - 2, first_row + rows - 3)
    cos_strip = [face_cosine(strip_row + p, lat_total) for p in range(4)]
    inv_strip = [1.0 / cell_cosine(strip_row + p, lat_total) for p in range(4)]

    def strip(which):
        low, high, last, first, inner = (ref[which] for ref in (below, above, to_north, to_south, third))
        halves = (
            (low[:levels], inner[levels:]),
            (low[levels:], last[:levels]),
            (first[:levels], last[levels:]),
            (first[levels:], high[:levels]),
            (inner[:levels], high[levels:]),
        )
        return [jnp.concatenate(pair, axis=0) for pair in halves]

    lat_strip = strip(2)
    lat_parts = [by_sign(0.5 * (lat_strip[p] + lat_strip[p + 1]), cos_strip[p]) for p in range(4)]
    lon_parts = [by_sign(values) for values in strip(3)]
    for which in range(2):
        start = strip(which)
        field = start
        for step in range(ITERS):
            moved = []
            flux = lat_parts[0][0] * field[0] + lat_parts[0][1] * field[1]
            for p in range(1, 4):
                before = flux
                moved.append(advance(
                    field[p], field[p + 1], lambda _: before,
                    *lon_parts[p], *lat_parts[p], inv_strip[p],
                ))
                flux = lat_parts[p][0] * field[p] + lat_parts[p][1] * field[p + 1]
            field = [inner_first[which], *moved, inner_first[which]]
        for p, side, row in ((2, 0, 0), (3, 0, 1), (1, 1, rows - 2), (2, 1, rows - 1)):
            tend = field[p] - start[p]
            done = start[p] + tend
            for level in range(levels):
                source = slice(side * levels + level, side * levels + level + 1)
                place = pl.ds(level * rows + (row - 8) % rows, 1)
                if which == 0:
                    thick_rows[place, :] = field[p][source]
                else:
                    tend_rows[place, :] = tend[source]
                    tracer_rows[place, :] = done[source]


def to_columns(source, target):
    for block in range(source.shape[1] // LANES):
        piece = pl.ds(block * LANES, LANES)
        target[piece, :] = source[:, piece].T


def add_damped(cut, tend, tables, tracer):
    half = tend.shape[0] // 2
    quarter = half // 2
    index = lax.broadcasted_iota(jnp.int32, (half, 1), 0)
    first, second = tend[pl.ds(0, half), :], tend[pl.ds(half, half), :]

    def times(stage, parity, columns):
        high = columns.astype(jnp.bfloat16)
        low = (columns - high.astype(jnp.float32)).astype(jnp.bfloat16)
        both = jnp.dot(tables[2 * stage, parity], jnp.concatenate([high, low], axis=1), preferred_element_type=jnp.float32)
        rest = jnp.dot(tables[2 * stage + 1, parity], high, preferred_element_type=jnp.float32)
        return both[:, :LANES] + (both[:, LANES:] + rest)

    changes = []
    for parity in range(2):
        if parity == 0:
            wave = jnp.where(index <= quarter, 2 * index, 2 * (index - quarter))
        else:
            wave = jnp.where(index < quarter, 2 * index + 1, 2 * (index - quarter) + 1)
        ratio = cut * (1.0 / jnp.maximum(wave, 1).astype(jnp.float32))
        damping = jnp.where(wave == 0, 1.0, jnp.minimum(1.0, ratio * ratio))
        coefficients = times(0, parity, first + second if parity == 0 else first - second)
        changes.append(times(1, parity, coefficients * (damping - 1.0)))
    tracer[pl.ds(0, half), :] += changes[0] + changes[1]
    tracer[pl.ds(half, half), :] += changes[0] - changes[1]


def prepare_weights(weights, fraction, fraction_cols):
    level_total, rows, dest = weights.shape
    levels = LANES // rows
    pieces = dest // 8

    def add(level, total):
        total = total + weights[level]
        fraction[level, :, pl.ds(0, dest)] = total.astype(jnp.float32)
        return total

    total = lax.fori_loop(0, level_total, add, jnp.zeros((rows, dest), jnp.int32), unroll=8)
    inverse = 1.0 / total.astype(jnp.float32)

    @pl.loop(0, level_total // levels)
    def _(group):
        here = pl.ds(group * levels, levels)
        fraction[here, :, pl.ds(0, dest)] = fraction[here, :, pl.ds(0, dest)] * inverse[None]
        columns = spread(fraction[here]).reshape(LANES, LANES).T
        for pair in range(pieces // 2):
            middle, outer = pair_up(columns[16 * pair : 16 * pair + 8], columns[16 * pair + 8 : 16 * pair + 16], rows)
            fraction_cols[group, pl.ds(8 * pair, 8), :] = middle
            fraction_cols[group, pl.ds(8 * (pieces // 2 + pair), 8), :] = outer
        if pieces % 2:
            fraction_cols[group, pl.ds(dest - 8, 8), :] = columns[dest - 8 : dest]


def interpolate(rows, piece, place, thick, tracer, fraction_cols, tops_turned, slopes_turned, below, mass_cols):
    sources = thick.shape[0]
    levels = LANES // rows
    groups = sources
    lane_level = lax.broadcasted_iota(jnp.int32, (8, LANES), 1) // rows
    there = pl.ds(pl.multiple_of(piece * 8, 8), 8)
    here = pl.ds(pl.multiple_of(place * 8, 8), 8)
    zero = jnp.zeros((8, LANES), jnp.float32)

    def turn(values, count):
        return pltpu.roll(values, count * rows, axis=1)

    carry = offset = last = zero
    for source in range(sources):
        layer = thick[source, there, :]
        ratio = tracer[source, there, :] / layer
        one = turn(layer, 1)
        two = layer + jnp.where(lane_level >= 1, one, 0.0)
        inclusive = two + jnp.where(lane_level >= 2, turn(two, 2), 0.0)
        pair = layer + one
        tops = carry + (inclusive - layer)
        carry = carry + (pair + turn(pair, 2))
        moved = turn(ratio, 1)
        slope = ratio - jnp.where(lane_level >= 1, moved, last)
        last = moved
        offset = offset + slope * tops
        for count in range(levels):
            tops_turned[source * levels + count] = turn(tops, count) if count else tops
            slopes_turned[source * levels + count] = turn(slope, count) if count else slope
    offset = offset + turn(offset, 1)
    offset = offset + turn(offset, 2)
    mass_cols[here, :] = carry
    targets = [carry * fraction_cols[group, here, :] for group in range(groups)]

    def accumulate(index, sums):
        tops, slope = tops_turned[index], slopes_turned[index]
        return tuple(s + slope * jnp.maximum(t, tops) for s, t in zip(sums, targets))

    sums = lax.fori_loop(0, sources * levels, accumulate, (zero,) * groups, unroll=4)
    for group in range(groups):
        below[group, here, :] = sums[group] - offset


def peers_of(n_lev, ring):
    lev = lax.axis_index("lev")
    planes = n_lev // ring
    hops = sorted(range(ring), key=lambda hop: -min(hop, ring - hop))
    return [
        lax.rem(lev // ring + plane, planes) * ring + lax.rem(lax.rem(lev, ring) + hop, ring)
        for hop in hops for plane in range(planes) if (plane, hop) != (0, 0)
    ]


def send(peers, source, target, sent, got, which, first, count):
    started = []
    lev = lax.axis_index("lev")
    for index, other in enumerate(peers):
        copy = pltpu.make_async_remote_copy(
            src_ref=source.at[other, pl.ds(first, count)], dst_ref=target.at[lev, pl.ds(first, count)],
            send_sem=sent.at[which, index], recv_sem=got.at[which, index],
            device_id={"lev": other}, device_id_type=MESH,
        )
        copy.start()
        started.append(copy)
    return started


def add_filter(cut_in, tend_rows, tend_cols, cut_lanes, tables, tracer):
    rows = cut_in.shape[1]
    to_columns(tend_rows, tend_cols)
    cut = spread_lanes(cut_in[...].astype(jnp.float32))
    for level in range(LANES // rows):
        cut_lanes[:, pl.ds(level * rows, rows)] = jnp.broadcast_to(cut, (8, rows))
    add_damped(cut_lanes[pl.ds(0, 1), :], tend_cols, tables, tracer)


def spread_lanes(values):
    return jnp.concatenate([values[:, 8:], values[:, :8]], axis=1)


def is_polar(n_lat):
    lat = lax.axis_index("lat")
    return (lat < 2) | (lat >= n_lat - 2)


def choose(columns, target, rows, part):
    n_lev, count, _ = target.shape
    dest = columns.shape[0] // n_lev
    pairs = dest // 16

    @pl.loop(0, n_lev)
    def _(other):
        for pair in range(pairs):
            start = other * dest + 16 * pair
            first = columns[pl.ds(pl.multiple_of(start, 8), 8), :]
            second = columns[pl.ds(pl.multiple_of(start + 8, 8), 8), :]
            target[other, pl.ds(8 * pair, 8), :] = pair_up(first, second, rows)[part]
        if count > 8 * pairs:
            target[other, pl.ds(8 * pairs, 8), :] = columns[pl.ds(pl.multiple_of(other * dest + 16 * pairs, 8), 8), :]


def step_kernel(
    n_lat, n_lev, ring, lat_total, chunks,
    thick_hbm, tracer_hbm, lon_hbm, lat_hbm, cut_hbm, weights_hbm, tables_hbm,
    below, fraction, mass_cols,
    cut_in, weights_in, tables, thick_in, tracer_in, lon_in, lat_in,
    thick_rows, tracer_rows, tend_rows, to_north, to_south, south_rows, north_rows, third, inner_first,
    columns, tend_cols, cut_lanes, thick_middle_send, tracer_middle_send, thick_middle, tracer_middle,
    thick_send, tracer_send, thick_cols, tracer_cols, fraction_cols, tops_turned, slopes_turned,
    load_sem, other_sem, ready, halo_sent, halo_got, middle_sent, middle_got, sent, got,
):
    levels, rows, _ = thick_in.shape
    middle, outer = thick_middle.shape[1], thick_cols.shape[1]
    lat, lev = lax.axis_index("lat"), lax.axis_index("lev")
    polar = is_polar(n_lat)
    odd = lax.rem(lat, 2)
    north, south = lax.rem(lat + 1, n_lat), lax.rem(lat + n_lat - 1, n_lat)
    peers = peers_of(n_lev, ring)
    barrier = pltpu.get_barrier_semaphore()
    for other in peers:
        pl.semaphore_signal(barrier, inc=1, device_id={"lev": other}, device_id_type=MESH)

    @pl.when(odd == 0)
    def _():
        for place in (north, south):
            pl.semaphore_signal(barrier, inc=1, device_id={"lat": place}, device_id_type=MESH)

    inputs = ((thick_hbm, thick_in), (tracer_hbm, tracer_in), (lat_hbm, lat_in), (lon_hbm, lon_in))

    def load(level):
        return [
            pltpu.make_async_copy(source.at[level], target.at[level], load_sem.at[level, i])
            for i, (source, target) in enumerate(inputs)
        ]

    def arrive(level):
        for copy in load(level):
            copy.wait()

    others = [
        pltpu.make_async_copy(source, target, other_sem.at[i])
        for i, (source, target) in enumerate(((weights_hbm, weights_in), (cut_hbm, cut_in), (tables_hbm, tables)))
    ]
    for level in range(levels):
        for copy in load(level):
            copy.start()
    for copy in others[:2]:
        copy.start()

    @pl.when(polar)
    def _():
        others[2].start()

    inner_rows(
        lat_total, (thick_in, tracer_in, lat_in, lon_in), arrive,
        thick_rows, tracer_rows, tend_rows, to_north, to_south, third, inner_first,
    )

    @pl.when(odd == 0)
    def _():
        pl.semaphore_wait(barrier, len(peers))

    @pl.when(odd == 1)
    def _():
        pl.semaphore_wait(barrier, len(peers) + 2)

    halos = [
        pltpu.make_async_remote_copy(
            src_ref=source, dst_ref=target, send_sem=halo_sent.at[side], recv_sem=halo_got.at[side],
            device_id={"lat": place}, device_id_type=MESH,
        )
        for side, (source, target, place) in enumerate(((to_north, south_rows, north), (to_south, north_rows, south)))
    ]

    @pl.when(odd == 1)
    def _():
        for side, place in enumerate((north, south)):
            pl.semaphore_signal(ready.at[side], inc=1, device_id={"lat": place}, device_id_type=MESH)
        for copy in halos:
            copy.start()

    to_columns(thick_rows, columns)
    choose(columns, thick_middle_send, rows, 0)
    thick_moving = send(peers, thick_middle_send, thick_middle, middle_sent, middle_got, 0, 0, middle)

    @pl.when(odd == 0)
    def _():
        for side in range(2):
            pl.semaphore_wait(ready.at[side], 1)
        for copy in halos:
            copy.start()

    to_columns(tracer_rows, columns)
    for copy in others[:2]:
        copy.wait()

    @pl.when(polar)
    def _():
        others[2].wait()
        add_filter(cut_in, tend_rows, tend_cols, cut_lanes, tables, columns)

    choose(columns, tracer_middle_send, rows, 0)
    tracer_moving = send(peers, tracer_middle_send, tracer_middle, middle_sent, middle_got, 1, 0, middle)
    thick_middle[lev] = thick_middle_send[lev]
    tracer_middle[lev] = tracer_middle_send[lev]
    for copy in halos:
        copy.wait()
    edges(
        lat_total, rows, south_rows, north_rows, to_north, to_south, third, inner_first, thick_rows, tracer_rows, tend_rows
    )
    to_columns(thick_rows, columns)
    choose(columns, thick_send, rows, 1)
    thick_copies = send(peers, thick_send, thick_cols, sent, got, 0, 0, outer)
    to_columns(tracer_rows, columns)

    @pl.when(polar)
    def _():
        add_filter(cut_in, tend_rows, tend_cols, cut_lanes, tables, columns)

    choose(columns, tracer_send, rows, 1)
    bounds = [sum(chunks[:i]) for i in range(len(chunks) + 1)]
    tracer_copies = [
        send(peers, tracer_send, tracer_cols, sent, got, 1 + i, 8 * bounds[i], 8 * chunks[i]) for i in range(len(chunks))
    ]
    thick_cols[lev] = thick_send[lev]
    tracer_cols[lev] = tracer_send[lev]
    prepare_weights(weights_in, fraction, fraction_cols)
    for copy in thick_moving + tracer_moving:
        copy.wait()

    @pl.loop(0, middle // 8)
    def _(piece):
        interpolate(
            rows, piece, piece, thick_middle, tracer_middle, fraction_cols, tops_turned, slopes_turned, below, mass_cols
        )

    for copy in thick_copies:
        copy.wait()
    for i in range(len(chunks)):
        for copy in tracer_copies[i]:
            copy.wait()

        @pl.loop(bounds[i], bounds[i + 1])
        def _(piece):
            interpolate(
                rows, piece, middle // 8 + piece, thick_cols, tracer_cols, fraction_cols, tops_turned, slopes_turned,
                below, mass_cols,
            )


def finish_kernel(below, fraction, mass_cols, thick_hbm, tracer_hbm, new_thick, new_tracer, sorted_cols, sems):
    groups = below.shape[0]
    levels, rows, dest = new_thick.shape[0] // groups, new_thick.shape[1], new_thick.shape[2]
    pieces = dest // 8
    low = lane_half(rows)

    def to_rows(source, slot):
        for pair in range(pieces // 2):
            middle = source[8 * pair : 8 * pair + 8]
            outer = source[8 * (pieces // 2 + pair) : 8 * (pieces // 2 + pair) + 8]
            sorted_cols[slot, pl.ds(16 * pair, 8), :] = jnp.where(low, middle, pltpu.roll(outer, rows // 2, axis=1))
            sorted_cols[slot, pl.ds(16 * pair + 8, 8), :] = jnp.where(low, pltpu.roll(middle, LANES - rows // 2, axis=1), outer)
        if pieces % 2:
            sorted_cols[slot, pl.ds(dest - 8, 8), :] = source[dest - 8 : dest]
        turned = sorted_cols[slot].T.reshape(levels, rows, LANES)
        return jnp.concatenate([turned[:, rows - 8 :], turned[:, : rows - 8]], axis=1)

    mass = to_rows(mass_cols[...], groups)[0, :, :dest]
    target_before = below_before = jnp.zeros((rows, dest), jnp.float32)
    copies = []

    def put(which, group, source, target):
        place = pl.ds(group * levels, levels)
        copy = pltpu.make_async_copy(source.at[place], target.at[place], sems.at[which, group])
        copy.start()
        copies.append(copy)

    for group in range(groups):
        block = to_rows(below[group], group)
        for inner in range(levels):
            level = group * levels + inner
            target = mass * fraction[level, :, pl.ds(0, dest)]
            new_thick[level] = target - target_before
            target_before = target
            now = block[inner, :, :dest]
            new_tracer[level] = now - below_before
            below_before = now
        put(0, group, new_thick, thick_hbm)
        put(1, group, new_tracer, tracer_hbm)
    for copy in copies:
        copy.wait()


def on_device(n_lat, n_lev, thickness, tracer_mass, courant_lon, courant_lat, filter_cut, target_weights):
    levels, rows, width = thickness.shape
    lat_total = n_lat * rows
    dest = width // n_lev
    level_total = target_weights.shape[0]
    groups = level_total * rows // LANES
    tables = jnp.asarray(fourier_tables(width))
    ring = min(n_lev, 8)
    pieces = dest // 8
    middle, outer = 8 * (pieces // 2), 8 * (pieces - pieces // 2)
    last = pieces - pieces // 2
    chunks = (last - last // 2 - 1, last // 2, 1)
    vmem, hbm = pl.BlockSpec(memory_space=pltpu.VMEM), pl.BlockSpec(memory_space=pltpu.HBM)
    f32, dma = jnp.float32, pltpu.SemaphoreType.DMA

    def in_hbm(*arrays):
        return [pltpu.with_memory_space_constraint(array, pltpu.HBM) for array in arrays]

    def scratch(kind, *shapes):
        return [pltpu.VMEM(shape, kind) for shape in shapes]

    def outs(*shapes):
        return tuple(jax.ShapeDtypeStruct(shape, f32) for shape in shapes)

    band = (LANES, width)
    pack = (4, 2 * levels, width)
    below, fraction, mass_cols = pl.pallas_call(
        functools.partial(step_kernel, n_lat, n_lev, ring, lat_total, chunks),
        out_shape=outs((groups, dest, LANES), (level_total, rows, LANES), (dest, LANES)),
        in_specs=[hbm] * 7,
        out_specs=(vmem,) * 3,
        scratch_shapes=scratch(jnp.int32, (1, rows), target_weights.shape)
        + scratch(jnp.bfloat16, tables.shape)
        + scratch(
            f32, *[thickness.shape] * 4, band, band, band, *[pack] * 5, (2, 2 * levels, width),
            (width, LANES), (width, LANES), (8, LANES),
            *[(n_lev, middle, LANES)] * 4, *[(n_lev, outer, LANES)] * 4, (groups, dest, LANES), *[(level_total, 8, LANES)] * 2,
        )
        + [dma((levels, 4)), dma((3,)), pltpu.SemaphoreType.REGULAR((2,)), dma((2,)), dma((2,))]
        + [dma((2, n_lev - 1))] * 2 + [dma((1 + len(chunks), n_lev - 1))] * 2,
        compiler_params=pltpu.CompilerParams(collective_id=0, has_side_effects=True, vmem_limit_bytes=32 << 20),
        name="step",
    )(*in_hbm(thickness, tracer_mass, courant_lon, courant_lat, filter_cut.reshape(1, rows), target_weights, tables))
    result = jax.ShapeDtypeStruct(target_weights.shape, f32)
    return pl.pallas_call(
        finish_kernel,
        out_shape=(result, result),
        in_specs=[vmem] * 3,
        out_specs=(hbm, hbm),
        scratch_shapes=scratch(f32, target_weights.shape, target_weights.shape, (groups + 1, LANES, LANES))
        + [dma((2, groups))],
        compiler_params=pltpu.CompilerParams(vmem_limit_bytes=16 << 20),
        name="finish",
    )(below, fraction, mass_cols)


def solution(mesh):
    n_lat, n_lev = mesh.shape["lat"], mesh.shape["lev"]
    placed = (
        P("lev", "lat", None),
        P("lev", "lat", None),
        P("lev", "lat", None),
        P("lev", "lat", None),
        P("lat"),
        P(None, "lat", "lev"),
    )
    return jax.shard_map(
        functools.partial(on_device, n_lat, n_lev),
        mesh=mesh,
        in_specs=placed,
        out_specs=(P(None, "lat", "lev"), P(None, "lat", "lev")),
        check_vma=False,
    )
```
